32 devices in a mesh: seq: 16 (over z, x, core), ch: 2 (over y).
Axes of the slice: x: 2, y: 2, z: 4, core: 2. Of those that a mesh axis runs over, the one named last changes fastest.
Arguments:
- queries: bfloat16 [4096, 4096], P('seq', 'ch'), may hold values from -6 to 6
- key_in: bfloat16 [4096, 4096], P('seq', 'ch'), may hold values from -6 to 6
- value_in: bfloat16 [4096, 4096], P('seq', 'ch'), may hold values from -6 to 6
- filter_raw: bfloat16 [4096, 4096], P('seq', 'ch'), may hold values from -6 to 6
- skip_gain: float32 [4096], P('ch'), may hold values from -4 to 4
- out_weight: bfloat16 [4096, 4096], P('ch'), may hold values from -0.09375 to 0.09375
- cotangent: bfloat16 [4096, 4096], P('seq', 'ch'), may hold values from -6 to 6
Outputs:
- projected: bfloat16 [4096, 4096], P('seq', 'ch')
- grad_query: bfloat16 [4096, 4096], P('seq', 'ch')
- grad_key: bfloat16 [4096, 4096], P('seq', 'ch')
- grad_value: bfloat16 [4096, 4096], P('seq', 'ch')
- grad_filter: bfloat16 [4096, 4096], P('seq', 'ch')
The draws below stay inside these ranges and needn't reach their ends.
All inputs are finite; a program needn't handle non-finite values.
Results may differ from the reference program's by a relative error of at most 0.015.
Values may be sent and summed in bfloat16 or wider, within the bound.
A program may use at most 192 MiB of HBM per device.

```python
import math
import jax
import jax.numpy as jnp
from jax import lax

WIDTH = 4096
SEQ = 4096


def shard_levels(rng, extent, pieces, low, top_value):
    factor_of = 1.0
    for position, parts in pieces:
        draws = jax.random.uniform(jax.random.fold_in(jax.random.fold_in(rng, 6), position), (parts,), jnp.float32, low / len(pieces), top_value / len(pieces))
        factor_of = factor_of * jnp.repeat(jnp.exp(draws), extent[position] // parts).reshape((-1,) + (1,) * (len(extent) - 1 - position))
    return factor_of


def gaussian(key, dims, scale, bound, pieces=(), dtype=jnp.bfloat16):
    factor_of = shard_levels(key, dims, pieces, -0.22, 0.18) if pieces else 1.0
    result = jax.random.normal(key, dims, jnp.float32) * scale * factor_of
    return jnp.minimum(jnp.maximum(result, -bound), bound).astype(dtype)


def setup_inputs(seed: int = 0) -> dict:
    keys = jax.random.split(jax.random.key(seed), 8)
    queries = gaussian(keys[0], (SEQ, WIDTH), 1.0, 6.0, ((0, 16), (1, 2)))
    key_in = gaussian(keys[1], (SEQ, WIDTH), 1.0, 6.0, ((0, 16), (1, 2)))
    value_in = gaussian(keys[2], (SEQ, WIDTH), 1.0, 6.0, ((0, 16), (1, 2)))
    filter_raw = gaussian(keys[3], (SEQ, WIDTH), 1.0, 6.0, ((0, 16), (1, 2)))
    skip_gain = gaussian(keys[4], (WIDTH,), 1.0, 4.0, ((0, 2),), jnp.float32)
    out_weight = gaussian(keys[5], (WIDTH, WIDTH), WIDTH ** -0.5, 0.09375, ((0, 2),))
    cotangent = gaussian(keys[6], (SEQ, WIDTH), 1.0, 6.0, ((0, 16), (1, 2)))
    return dict(queries=queries, key_in=key_in, value_in=value_in, filter_raw=filter_raw, skip_gain=skip_gain, out_weight=out_weight, cotangent=cotangent)


def spectral_group(arrays):
    product_kv, filter_raw, grad_conv = arrays
    length = 2 * SEQ
    z_freq = jnp.fft.rfft(product_kv, n=length, axis=0)
    h_freq = jnp.fft.rfft(filter_raw, n=length, axis=0)
    g_freq = jnp.fft.rfft(grad_conv, n=length, axis=0)
    forward_part = jnp.fft.irfft(h_freq * z_freq, n=length, axis=0)[:SEQ]
    backward_part = jnp.fft.irfft(jnp.conj(h_freq) * g_freq, n=length, axis=0)[:SEQ]
    filter_part = jnp.fft.irfft(jnp.conj(z_freq) * g_freq, n=length, axis=0)[:SEQ]
    return (forward_part, backward_part, filter_part)

def reference(queries, key_in, value_in, filter_raw, skip_gain, out_weight, cotangent):
    product_kv = (key_in.astype(jnp.float32) * value_in.astype(jnp.float32)).astype(jnp.bfloat16)
    grad_mixed = jnp.dot(cotangent, out_weight.T, preferred_element_type=jnp.float32)
    grad_conv = (grad_mixed * queries.astype(jnp.float32)).astype(jnp.bfloat16)
    group_width = math.gcd(WIDTH, 256)
    groups = WIDTH // group_width

    def to_groups(array):
        return array.astype(jnp.float32).reshape(SEQ, groups, group_width).transpose(1, 0, 2)

    def from_groups(array):
        return array.transpose(1, 0, 2).reshape(SEQ, WIDTH)
    results = lax.map(spectral_group, (to_groups(product_kv), to_groups(filter_raw), to_groups(grad_conv)))
    factor = 1.0 / math.sqrt(SEQ)
    forward_part = from_groups(results[0]) * factor
    backward_part = from_groups(results[1]) * factor
    filter_part = from_groups(results[2]) * factor
    skip_values = skip_gain.astype(jnp.float32)
    convolved = forward_part + skip_values * product_kv.astype(jnp.float32)
    gated_output = (queries.astype(jnp.float32) * convolved).astype(jnp.bfloat16)
    projected = jnp.dot(gated_output, out_weight, preferred_element_type=jnp.float32).astype(jnp.bfloat16)
    grad_query = (grad_mixed * convolved).astype(jnp.bfloat16)
    grad_product = backward_part + skip_values * grad_conv.astype(jnp.float32)
    grad_key = (grad_product * value_in.astype(jnp.float32)).astype(jnp.bfloat16)
    grad_value = (grad_product * key_in.astype(jnp.float32)).astype(jnp.bfloat16)
    grad_filter = filter_part.astype(jnp.bfloat16)
    return (projected, grad_query, grad_key, grad_value, grad_filter)
```

```python
import math

import jax
import jax.numpy as jnp
import numpy as np
from jax import lax
from jax.sharding import PartitionSpec as P

bf16 = jnp.bfloat16
f32 = jnp.float32


def split_period(period):
    second = 1 << ((period.bit_length() - 1) // 2)
    return period // second, second


def outer_table(first):
    f1 = np.arange(first // 2 + 1)[:, None]
    a = np.arange(first // 2)[None, :]
    angles = (f1 * a % first) * (2.0 * math.pi / first)
    return np.stack([np.cos(angles), -np.sin(angles)])


def inner_table(first, second):
    period = first * second
    f1 = np.arange(first // 2 + 1)[:, None, None]
    f2 = np.arange(second)[None, :, None]
    b = np.arange(second)[None, None, :]
    angles = (b * (f1 + first * f2) % period) * (2.0 * math.pi / period)
    cosine, sine = np.cos(angles), np.sin(angles)
    top = np.stack([cosine, sine], axis=2)
    bottom = np.stack([-sine, cosine], axis=2)
    return np.stack([top, bottom], axis=1)


def forward(signal, outer, inner):
    count, length, width = signal.shape
    pieces = signal.reshape(count, outer.shape[2], inner.shape[4], width)
    mid = jnp.einsum("pfa,sabc->fpbsc", outer, pieces, preferred_element_type=f32)
    mid = mid.astype(bf16)
    return jnp.einsum("fqgpb,fpbsc->fqgsc", inner, mid, preferred_element_type=f32)


def inverse(spectra, outer, inner):
    count, width = spectra.shape[3:]
    mid = jnp.einsum("fqgpb,fqgsc->fpbsc", inner, spectra, preferred_element_type=f32)
    mid = mid.astype(bf16)
    out = jnp.einsum("pfa,fpbsc->sabc", outer, mid, preferred_element_type=f32)
    return out.reshape(count, -1, width)


def to_channels(signals):
    devices = lax.axis_size("seq")
    count, rows, width = signals.shape
    parts = signals.reshape(count, rows, devices, width // devices).transpose(2, 0, 1, 3)
    parts = lax.all_to_all(parts, "seq", split_axis=0, concat_axis=0, tiled=True)
    return parts.transpose(1, 0, 2, 3).reshape(count, devices * rows, width // devices)


def to_positions(signals):
    devices = lax.axis_size("seq")
    count, length, width = signals.shape
    parts = signals.reshape(count, devices, length // devices, width).transpose(1, 0, 2, 3)
    parts = lax.all_to_all(parts, "seq", split_axis=0, concat_axis=0, tiled=True)
    return parts.transpose(1, 2, 0, 3).reshape(count, length // devices, devices * width)


def shifted(value, shift):
    size = lax.axis_size("ch")
    return lax.ppermute(value, "ch", [(i, (i + shift) % size) for i in range(size)])


def gather_columns(value):
    size, me = lax.axis_size("ch"), lax.axis_index("ch")
    rows, width = value.shape
    full = jnp.zeros((rows, size * width), value.dtype)
    for shift in range(size):
        part = shifted(value, shift) if shift else value
        owner = (me - shift + size) % size
        full = lax.dynamic_update_slice(full, part, (0, owner * width))
    return full


def scatter_columns(value):
    size, me = lax.axis_size("ch"), lax.axis_index("ch")
    rows, width = value.shape[0], value.shape[1] // size
    total = lax.dynamic_slice(value, (0, me * width), (rows, width))
    for shift in range(1, size):
        target = (me + shift) % size
        part = lax.dynamic_slice(value, (0, target * width), (rows, width)).astype(bf16)
        total = total + shifted(part, shift).astype(f32)
    return total


def on_device(queries, key_in, value_in, filter_raw, skip_gain, out_weight, cotangent):
    local_rows, local_width = queries.shape
    seq_devices = lax.axis_size("seq")
    length = local_rows * seq_devices
    group = local_width // seq_devices
    first, second = split_period(2 * length)
    table = outer_table(first)
    weight = np.full((first // 2 + 1, 1), 2.0)
    weight[0] = weight[-1] = 1.0
    outer = jnp.asarray(table, bf16)
    outer_back = jnp.asarray(table * weight, bf16)
    inner = jnp.asarray(inner_table(first, second).astype(jnp.bfloat16))
    factor = 1.0 / (math.sqrt(length) * 2.0 * length)
    skip_part = lax.dynamic_slice(skip_gain, (lax.axis_index("seq") * group,), (group,))

    product_kv = (key_in.astype(f32) * value_in.astype(f32)).astype(bf16)
    held = to_channels(jnp.stack([product_kv, filter_raw]))

    grad_mixed = lax.dot_general(
        gather_columns(cotangent),
        out_weight,
        (((1,), (1,)), ((), ())),
        preferred_element_type=f32,
    )
    grad_conv = (grad_mixed * queries.astype(f32)).astype(bf16)
    held_grad = to_channels(grad_conv[None])

    both = forward(held, outer, inner)
    zr, zi = both[:, 0, :, 0], both[:, 1, :, 0]
    hr, hi = both[:, 0, :, 1], both[:, 1, :, 1]
    conv = jnp.stack([hr * zr - hi * zi, hr * zi + hi * zr], axis=1).astype(bf16)
    conv = inverse(conv[:, :, :, None], outer_back, inner) * factor
    conv = (conv + skip_part * held[:1].astype(f32)).astype(bf16)
    convolved = to_positions(conv)[0].astype(f32)

    grad = forward(held_grad, outer, inner)
    gr, gi = grad[:, 0, :, 0], grad[:, 1, :, 0]
    back = jnp.stack([hr * gr + hi * gi, hr * gi - hi * gr], axis=1)
    taps = jnp.stack([zr * gr + zi * gi, zr * gi - zi * gr], axis=1)
    two = inverse(jnp.stack([back, taps], axis=3).astype(bf16), outer_back, inner) * factor
    back = two[0] + skip_part * held_grad[0].astype(f32)
    two = to_positions(jnp.stack([back, two[1]]).astype(bf16))

    gated_output = (queries.astype(f32) * convolved).astype(bf16)
    partial_terms = jnp.dot(gated_output, out_weight, preferred_element_type=f32)
    projected = scatter_columns(partial_terms).astype(bf16)
    grad_query = (grad_mixed * convolved).astype(bf16)
    grad_product = two[0].astype(f32)
    grad_key = (grad_product * value_in.astype(f32)).astype(bf16)
    grad_value = (grad_product * key_in.astype(f32)).astype(bf16)
    return (projected, grad_query, grad_key, grad_value, two[1])


def solution(mesh):
    placed = (
        P("seq", "ch"),
        P("seq", "ch"),
        P("seq", "ch"),
        P("seq", "ch"),
        P("ch"),
        P("ch", None),
        P("seq", "ch"),
    )
    return jax.shard_map(
        on_device,
        mesh=mesh,
        in_specs=placed,
        out_specs=(P("seq", "ch"),) * 5,
        check_vma=False,
    )
```

```python
import math

import jax
import jax.numpy as jnp
import numpy as np
from jax import lax
from jax.experimental import pallas as pl
from jax.sharding import PartitionSpec as P


bf16 = jnp.bfloat16
f32 = jnp.float32


def split_period(period):
    second = 1 << ((period.bit_length() - 1) // 2)
    return period // second, second


def outer_table(first):
    f1 = np.arange(first // 2 + 1)[:, None]
    a = np.arange(first // 2)[None, :]
    angles = (f1 * a % first) * (2.0 * math.pi / first)
    return np.stack([np.cos(angles), -np.sin(angles)])


def inner_table(first, second):
    period = first * second
    f1 = np.arange(first // 2 + 1)[:, None, None]
    f2 = np.arange(second)[None, :, None]
    b = np.arange(second)[None, None, :]
    angles = (b * (f1 + first * f2) % period) * (2.0 * math.pi / period)
    cosine, sine = np.cos(angles), np.sin(angles)
    top = np.concatenate([cosine, sine], axis=2)
    bottom = np.concatenate([-sine, cosine], axis=2)
    return np.concatenate([top, bottom], axis=1)


def forward(signal, outer, inner):
    count, _, width = signal.shape
    second = inner.shape[2] // 2
    pieces = signal.reshape(count, outer.shape[2], second, width)
    mid = jnp.einsum("pfa,sabc->fpbsc", outer, pieces, preferred_element_type=f32)
    mid = mid.astype(bf16).reshape(-1, 2 * second, count, width)
    return jnp.einsum("fxy,fysc->fxsc", inner, mid, preferred_element_type=f32)


def inverse(spectra, outer, inner):
    freqs, double, count, width = spectra.shape
    mid = jnp.einsum("fxy,fxsc->fysc", inner, spectra, preferred_element_type=f32)
    mid = mid.astype(bf16).reshape(freqs, 2, double // 2, count, width)
    out = jnp.einsum("pfa,fpbsc->sabc", outer, mid, preferred_element_type=f32)
    return out.reshape(count, -1, width)


def exchange(value):
    return lax.all_to_all(value, "seq", split_axis=0, concat_axis=0, tiled=True)


def grouped(body, wide, tall, wide_out, tall_out):
    rows = (wide[0] if wide else tall[0]).shape[0 if wide else 2]
    width = wide[0].shape[1] // lax.axis_size("seq") if wide else tall[0].shape[3]
    groups = lax.axis_size("seq")
    if width % 128:
        wide_tiles = [
            [v[:, i * width : (i + 1) * width] for v in wide] for i in range(groups)
        ]
        results = [
            body(wide_tiles[i], [[v[i, k] for k in range(v.shape[1])] for v in tall])
            for i in range(groups)
        ]
        outs = [
            jnp.concatenate([r[0][j] for r in results], axis=1).astype(t)
            for j, t in enumerate(wide_out)
        ]
        outs += [
            jnp.stack([jnp.stack(r[1][j]) for r in results]).astype(t)
            for j, (_, t) in enumerate(tall_out)
        ]
        return outs
    step = math.gcd(groups, 4)

    def kernel(*refs):
        wide_in = refs[: len(wide)]
        tall_in = refs[len(wide) : len(wide) + len(tall)]
        outs = refs[len(wide) + len(tall) :]
        for i in range(step):
            lanes = slice(i * width, (i + 1) * width)
            flat, stacked = body(
                [r[:, lanes] for r in wide_in],
                [[r[i, k] for k in range(r.shape[1])] for r in tall_in],
            )
            for ref, value in zip(outs, flat):
                ref[:, lanes] = value.astype(ref.dtype)
            for ref, kinds in zip(outs[len(flat) :], stacked):
                for k, value in enumerate(kinds):
                    ref[i, k] = value.astype(ref.dtype)

    flat_spec = pl.BlockSpec((rows, step * width), lambda i: (0, i))

    def tall_spec(kinds):
        return pl.BlockSpec((step, kinds, rows, width), lambda i: (i, 0, 0, 0))

    shapes = [jax.ShapeDtypeStruct((rows, groups * width), t) for t in wide_out]
    shapes += [jax.ShapeDtypeStruct((groups, n, rows, width), t) for n, t in tall_out]
    moved = sum(v.size * v.dtype.itemsize for v in [*wide, *tall])
    moved += sum(math.prod(v.shape) * v.dtype.itemsize for v in shapes)
    return pl.pallas_call(
        kernel,
        grid=(groups // step,),
        in_specs=[flat_spec] * len(wide) + [tall_spec(v.shape[1]) for v in tall],
        out_specs=[flat_spec] * len(wide_out) + [tall_spec(n) for n, _ in tall_out],
        out_shape=shapes,
        cost_estimate=pl.CostEstimate(
            flops=rows * groups * width * 8, bytes_accessed=moved, transcendentals=0
        ),
    )(*wide, *tall)


def pack_inputs(tiles, _):
    key, value, taps = tiles
    product = key.astype(f32) * value.astype(f32)
    return [], [[product.astype(bf16), taps]]


def pack_gradient(tiles, _):
    mixed, queries = tiles
    return [], [[mixed * queries.astype(f32)]]


def unpack_convolved(tiles, tall):
    mixed, queries = tiles
    convolved = tall[0][0].astype(f32)
    return [queries.astype(f32) * convolved, mixed * convolved], []


def unpack_gradients(tiles, tall):
    key, value = tiles
    back, taps = tall[0]
    back = back.astype(f32)
    return [back * value.astype(f32), back * key.astype(f32), taps], []


def shifted(value, shift):
    size = lax.axis_size("ch")
    return lax.ppermute(value, "ch", [(i, (i + shift) % size) for i in range(size)])


def gather_columns(value):
    size, me = lax.axis_size("ch"), lax.axis_index("ch")
    rows, width = value.shape
    full = jnp.zeros((rows, size * width), value.dtype)
    for shift in range(size):
        part = shifted(value, shift) if shift else value
        owner = (me - shift + size) % size
        full = lax.dynamic_update_slice(full, part, (0, owner * width))
    return full


def scatter_columns(value):
    size, me = lax.axis_size("ch"), lax.axis_index("ch")
    rows, width = value.shape[0], value.shape[1] // size
    total = lax.dynamic_slice(value, (0, me * width), (rows, width))
    for shift in range(1, size):
        target = (me + shift) % size
        part = lax.dynamic_slice(value, (0, target * width), (rows, width)).astype(bf16)
        total = total + shifted(part, shift).astype(f32)
    return total


def on_device(queries, key_in, value_in, filter_raw, skip_gain, out_weight, cotangent):
    local_rows, local_width = queries.shape
    seq_devices = lax.axis_size("seq")
    length = local_rows * seq_devices
    group = local_width // seq_devices
    first, second = split_period(2 * length)
    table = outer_table(first)
    weight = np.full((first // 2 + 1, 1), 2.0)
    weight[0] = weight[-1] = 1.0
    outer = jnp.asarray(table, bf16)
    outer_back = jnp.asarray(table * weight, bf16)
    inner = lax.optimization_barrier(jnp.asarray(inner_table(first, second), bf16))
    factor = 1.0 / (math.sqrt(length) * 2.0 * length)
    skip_part = lax.dynamic_slice(skip_gain, (lax.axis_index("seq") * group,), (group,))

    def held_form(parts):
        return parts.transpose(1, 0, 2, 3).reshape(parts.shape[1], length, group)

    def sent_form(values):
        kinds = values.shape[0]
        return values.reshape(kinds, seq_devices, local_rows, group).transpose(1, 0, 2, 3)

    (sent,) = grouped(pack_inputs, [key_in, value_in, filter_raw], [], [], [(2, bf16)])
    got = exchange(sent)
    held = held_form(got)

    gathered = gather_columns(cotangent)
    grad_mixed = lax.dot_general(
        gathered, out_weight, (((1,), (1,)), ((), ())), preferred_element_type=f32
    )
    (sent,) = grouped(pack_gradient, [grad_mixed, queries], [], [], [(1, bf16)])
    got = exchange(sent)
    held_grad = held_form(got)

    both = forward(held, outer, inner)
    zr, zi = both[:, :second, 0], both[:, second:, 0]
    hr, hi = both[:, :second, 1], both[:, second:, 1]
    conv = jnp.concatenate([hr * zr - hi * zi, hr * zi + hi * zr], axis=1).astype(bf16)
    conv = inverse(conv[:, :, None], outer_back, inner) * factor
    conv = (conv + skip_part * held[:1].astype(f32)).astype(bf16)
    convolved = exchange(sent_form(conv))

    grad = forward(held_grad, outer, inner)
    zr, zi, hr, hi = lax.optimization_barrier((zr, zi, hr, hi))
    gr, gi = grad[:, :second, 0], grad[:, second:, 0]
    back = jnp.concatenate([hr * gr + hi * gi, hr * gi - hi * gr], axis=1)
    taps = jnp.concatenate([zr * gr + zi * gi, zr * gi - zi * gr], axis=1)
    two = inverse(jnp.stack([back, taps], axis=2).astype(bf16), outer_back, inner) * factor
    back = two[0] + skip_part * held_grad[0].astype(f32)
    two = sent_form(jnp.stack([back, two[1]]).astype(bf16))
    two = exchange(two)

    gated_output, grad_query = grouped(
        unpack_convolved, [grad_mixed, queries], [convolved], [bf16, bf16], []
    )
    partial_terms = jnp.dot(gated_output, out_weight, preferred_element_type=f32)
    projected = scatter_columns(partial_terms).astype(bf16)
    grad_key, grad_value, grad_filter = grouped(
        unpack_gradients, [key_in, value_in], [two], [bf16, bf16, bf16], []
    )
    return (projected, grad_query, grad_key, grad_value, grad_filter)


def solution(mesh):
    placed = (
        P("seq", "ch"),
        P("seq", "ch"),
        P("seq", "ch"),
        P("seq", "ch"),
        P("ch"),
        P("ch", None),
        P("seq", "ch"),
    )
    return jax.shard_map(
        on_device,
        mesh=mesh,
        in_specs=placed,
        out_specs=(P("seq", "ch"),) * 5,
        check_vma=False,
    )
```

```python
import math

import jax
import jax.numpy as jnp
import numpy as np
from jax import lax
from jax.experimental import pallas as pl
from jax.sharding import PartitionSpec as P


bf16 = jnp.bfloat16
f32 = jnp.float32


def split_period(period):
    second = 1 << ((period.bit_length() - 1) // 2)
    return period // second, second


def outer_table(first):
    f1 = np.arange(first // 2 + 1)[:, None]
    a = np.arange(first // 2)[None, :]
    angles = (f1 * a % first) * (2.0 * math.pi / first)
    return np.stack([np.cos(angles), -np.sin(angles)])


def inner_table(first, second):
    period = first * second
    f1 = np.arange(first // 2 + 1)[:, None]
    f2 = np.arange(second)[:, None]
    b = np.arange(second)[None, :]
    slow = (b * f1 % period) * (2.0 * math.pi / period)
    fast = (b * f2 % second) * (2.0 * math.pi / second)
    cosine, sine = np.cos(fast), np.sin(fast)
    small = (
        np.tile(np.cos(slow), 2),
        np.tile(np.sin(slow), 2),
        np.block([[cosine, sine], [-sine, cosine]]),
        np.block([[-sine, cosine], [-cosine, -sine]]),
    )
    small = lax.optimization_barrier(tuple(jnp.asarray(v, f32) for v in small))
    by_cosine, by_sine = small[0][:, None], small[1][:, None]
    table = (by_cosine * small[2][None] + by_sine * small[3][None]).astype(bf16)
    return lax.optimization_barrier(table)


def forward(signal, outer, inner):
    count, _, width = signal.shape
    second = inner.shape[2] // 2
    pieces = signal.reshape(count, outer.shape[2], second, width)
    mid = jnp.einsum("pfa,sabc->fpbsc", outer, pieces, preferred_element_type=f32)
    mid = mid.astype(bf16).reshape(-1, 2 * second, count, width)
    return jnp.einsum("fxy,fysc->fxsc", inner, mid, preferred_element_type=f32)


def inverse(spectra, outer, inner):
    freqs, double, count, width = spectra.shape
    mid = jnp.einsum("fxy,fxsc->fysc", inner, spectra, preferred_element_type=f32)
    mid = mid.astype(bf16).reshape(freqs, 2, double // 2, count, width)
    out = jnp.einsum("pfa,fpbsc->sabc", outer, mid, preferred_element_type=f32)
    return out.reshape(count, -1, width)


def exchange(value):
    return lax.all_to_all(value, "seq", split_axis=0, concat_axis=0, tiled=True)


def grouped(body, wide, tall, wide_out, tall_out):
    rows = (wide[0] if wide else tall[0]).shape[0 if wide else 2]
    width = wide[0].shape[1] // lax.axis_size("seq") if wide else tall[0].shape[3]
    groups = lax.axis_size("seq")
    if width % 128:
        wide_tiles = [
            [v[:, i * width : (i + 1) * width] for v in wide] for i in range(groups)
        ]
        results = [
            body(wide_tiles[i], [[v[i, k] for k in range(v.shape[1])] for v in tall])
            for i in range(groups)
        ]
        outs = [
            jnp.concatenate([r[0][j] for r in results], axis=1).astype(t)
            for j, t in enumerate(wide_out)
        ]
        outs += [
            jnp.stack([jnp.stack(r[1][j]) for r in results]).astype(t)
            for j, (_, t) in enumerate(tall_out)
        ]
        return outs
    step = math.gcd(groups, 4)

    def kernel(*refs):
        wide_in = refs[: len(wide)]
        tall_in = refs[len(wide) : len(wide) + len(tall)]
        outs = refs[len(wide) + len(tall) :]
        for i in range(step):
            lanes = slice(i * width, (i + 1) * width)
            flat, stacked = body(
                [r[:, lanes] for r in wide_in],
                [[r[i, k] for k in range(r.shape[1])] for r in tall_in],
            )
            for ref, value in zip(outs, flat):
                ref[:, lanes] = value.astype(ref.dtype)
            for ref, kinds in zip(outs[len(flat) :], stacked):
                for k, value in enumerate(kinds):
                    ref[i, k] = value.astype(ref.dtype)

    flat_spec = pl.BlockSpec((rows, step * width), lambda i: (0, i))

    def tall_spec(kinds):
        return pl.BlockSpec((step, kinds, rows, width), lambda i: (i, 0, 0, 0))

    shapes = [jax.ShapeDtypeStruct((rows, groups * width), t) for t in wide_out]
    shapes += [jax.ShapeDtypeStruct((groups, n, rows, width), t) for n, t in tall_out]
    moved = sum(v.size * v.dtype.itemsize for v in [*wide, *tall])
    moved += sum(math.prod(v.shape) * v.dtype.itemsize for v in shapes)
    return pl.pallas_call(
        kernel,
        grid=(groups // step,),
        in_specs=[flat_spec] * len(wide) + [tall_spec(v.shape[1]) for v in tall],
        out_specs=[flat_spec] * len(wide_out) + [tall_spec(n) for n, _ in tall_out],
        out_shape=shapes,
        cost_estimate=pl.CostEstimate(
            flops=rows * groups * width * 8, bytes_accessed=moved, transcendentals=0
        ),
    )(*wide, *tall)


def pack_inputs(tiles, _):
    key, value, taps = tiles
    product = key.astype(f32) * value.astype(f32)
    return [], [[product.astype(bf16), taps]]


def pack_gradient(tiles, _):
    mixed, queries = tiles
    return [], [[mixed * queries.astype(f32)]]


def unpack_convolved(tiles, tall):
    mixed, queries = tiles
    convolved = tall[0][0].astype(f32)
    return [queries.astype(f32) * convolved, mixed * convolved], []


def unpack_gradients(tiles, tall):
    key, value = tiles
    back, taps = tall[0]
    back = back.astype(f32)
    return [back * value.astype(f32), back * key.astype(f32), taps], []


def shifted(value, shift):
    size = lax.axis_size("ch")
    return lax.ppermute(value, "ch", [(i, (i + shift) % size) for i in range(size)])


def mixed_gradient(cotangent, out_weight):
    size, me = lax.axis_size("ch"), lax.axis_index("ch")
    width = cotangent.shape[1]
    total = None
    for shift in range(size):
        part = shifted(cotangent, shift) if shift else cotangent
        owner = (me - shift + size) % size
        weight = lax.dynamic_slice_in_dim(out_weight, owner * width, width, 1)
        term = lax.dot_general(
            part, weight, (((1,), (1,)), ((), ())), preferred_element_type=f32
        )
        total = term if total is None else total + term
    return total


def projection(gated, out_weight):
    size, me = lax.axis_size("ch"), lax.axis_index("ch")
    width = out_weight.shape[1] // size

    def columns(target):
        weight = lax.dynamic_slice_in_dim(out_weight, target * width, width, 1)
        return jnp.dot(gated, weight, preferred_element_type=f32)

    arrived = []
    for shift in range(1, size):
        part = columns((me + shift) % size).astype(bf16)
        arrived.append(shifted(part, shift))
    total = lax.optimization_barrier(columns(me))
    for part in arrived:
        total = total + part.astype(f32)
    return total.astype(bf16)


def on_device(queries, key_in, value_in, filter_raw, skip_gain, out_weight, cotangent):
    local_rows, local_width = queries.shape
    seq_devices = lax.axis_size("seq")
    length = local_rows * seq_devices
    group = local_width // seq_devices
    first, second = split_period(2 * length)
    table = outer_table(first)
    weight = np.full((first // 2 + 1, 1), 2.0)
    weight[0] = weight[-1] = 1.0
    outer = jnp.asarray(table, bf16)
    outer_back = jnp.asarray(table * weight, bf16)
    inner = inner_table(first, second)
    factor = 1.0 / (math.sqrt(length) * 2.0 * length)
    skip_part = lax.dynamic_slice(skip_gain, (lax.axis_index("seq") * group,), (group,))

    def held_form(parts):
        return parts.transpose(1, 0, 2, 3).reshape(parts.shape[1], length, group)

    def sent_form(values):
        kinds = values.shape[0]
        return values.reshape(kinds, seq_devices, local_rows, group).transpose(1, 0, 2, 3)

    (sent,) = grouped(pack_inputs, [key_in, value_in, filter_raw], [], [], [(2, bf16)])
    got = exchange(sent)
    held = held_form(got)

    grad_mixed = mixed_gradient(cotangent, out_weight)
    (sent,) = grouped(pack_gradient, [grad_mixed, queries], [], [], [(1, bf16)])
    got = exchange(sent)
    held_grad = held_form(got)

    both = forward(held, outer, inner)
    zr, zi = both[:, :second, 0], both[:, second:, 0]
    hr, hi = both[:, :second, 1], both[:, second:, 1]
    conv = jnp.concatenate([hr * zr - hi * zi, hr * zi + hi * zr], axis=1).astype(bf16)
    conv = inverse(conv[:, :, None], outer_back, inner) * factor
    conv = (conv + skip_part * held[:1].astype(f32)).astype(bf16)
    convolved = exchange(sent_form(conv))

    grad = forward(held_grad, outer, inner)
    zr, zi, hr, hi = lax.optimization_barrier((zr, zi, hr, hi))
    gr, gi = grad[:, :second, 0], grad[:, second:, 0]
    back = jnp.concatenate([hr * gr + hi * gi, hr * gi - hi * gr], axis=1)
    taps = jnp.concatenate([zr * gr + zi * gi, zr * gi - zi * gr], axis=1)
    two = inverse(jnp.stack([back, taps], axis=2).astype(bf16), outer_back, inner) * factor
    back = two[0] + skip_part * held_grad[0].astype(f32)
    two = sent_form(jnp.stack([back, two[1]]).astype(bf16))
    two = exchange(two)

    gated_output, grad_query = grouped(
        unpack_convolved, [grad_mixed, queries], [convolved], [bf16, bf16], []
    )
    projected = projection(gated_output, out_weight)
    grad_key, grad_value, grad_filter = grouped(
        unpack_gradients, [key_in, value_in], [two], [bf16, bf16, bf16], []
    )
    return (projected, grad_query, grad_key, grad_value, grad_filter)


def solution(mesh):
    placed = (
        P("seq", "ch"),
        P("seq", "ch"),
        P("seq", "ch"),
        P("seq", "ch"),
        P("ch"),
        P("ch", None),
        P("seq", "ch"),
    )
    return jax.shard_map(
        on_device,
        mesh=mesh,
        in_specs=placed,
        out_specs=(P("seq", "ch"),) * 5,
        check_vma=False,
    )
```
